256 devices in a mesh: expert: 64 (over z, x, core), dp: 4 (over y).
Axes of the slice: x: 4, y: 4, z: 8, core: 2. Of those that a mesh axis runs over, the one named last changes fastest.
Arguments:
- tokens: bfloat16 [32768, 2048], P(('expert', 'dp')), may hold values from -6 to 6
- cotangent: bfloat16 [32768, 2048], P(('expert', 'dp')), may hold values from -6 to 6
- expert_ids: int32 [32768, 4], P(('expert', 'dp')), may hold values from 0 to 63, all different within a row; in each aligned block of 128 rows (0 to 127, 128 to 255, ...) at most 9 rows name the same one
- gate_probs: float32 [32768, 4], P(('expert', 'dp')), may hold values from 0.05 to 1
- w_gate: bfloat16 [64, 2048, 768], P('expert', 'dp'), may hold values from -0.125 to 0.125
- w_up: bfloat16 [64, 2048, 768], P('expert', 'dp'), may hold values from -0.125 to 0.125
- w_down: bfloat16 [64, 768, 2048], P('expert', 'dp'), may hold values from -0.21875 to 0.21875
Outputs:
- grad_tokens: bfloat16 [32768, 2048], P(('expert', 'dp'))
- grad_gate: bfloat16 [64, 2048, 768], P('expert', 'dp')
- grad_up: bfloat16 [64, 2048, 768], P('expert', 'dp')
- grad_down: bfloat16 [64, 768, 2048], P('expert', 'dp')
The draws below stay inside these ranges and needn't reach their ends.
Inputs may be any that keep to these rules, and one draw needn't show every extreme that they name: `expert_ids`: the 4 experts of a token differ. Among the rows of one device no expert is named more than 9 times, a bound that some block reaches.
All inputs are finite; a program needn't handle non-finite values.
Results may differ from the reference program's by a relative error of at most 0.0064.
Values may be sent and summed in bfloat16 or wider, within the bound.
A program may use at most 128 MiB of HBM per device.

```python
import math
import jax
import jax.numpy as jnp
import numpy as np
from jax import lax

D = 2048
FF = 768
TOPK = 4
TOK_DEV = 128
EXPERTS = 64
TOKENS = 32768
CAP = 9
DEVICES = 256


def shard_levels(own_key, extent, pieces, low, largest):
    level = 1.0
    for dim, parts in pieces:
        draws = jax.random.uniform(jax.random.fold_in(jax.random.fold_in(own_key, 6), dim), (parts,), jnp.float32, low / len(pieces), largest / len(pieces))
        level = level * jnp.repeat(jnp.exp(draws), extent[dim] // parts).reshape((-1,) + (1,) * (len(extent) - 1 - dim))
    return level


def assign_block(rng, own, number, rows, number_of, top, most, lean):
    sequence = jax.random.permutation(rng, number_of)
    crowded, ordinary = portions_of(number_of, rows * top, most, lean, True), portions_of(number_of, rows * top, most, lean, False)
    places = jnp.arange(number_of)

    def named(lengths, offset_by):
        used = int((lengths > 0).sum())
        fixed = max(1, used // 4)
        moved = fixed + (places - fixed + offset_by * (used - fixed)) % max(1, number_of - fixed)
        return jnp.zeros((number_of,), jnp.int32).at[sequence[jnp.where(places < fixed, places, moved)]].set(jnp.asarray(lengths, jnp.int32))

    lengths = jnp.where(number % 4 == 0, named(crowded, number // 4), named(ordinary, number - number // 4 - 1))
    mixed = jax.random.permutation(jax.random.fold_in(own, 3), number_of)
    source_of, taker = mixed[0:number_of // 2 * 2:2], mixed[1:number_of // 2 * 2:2]
    slack = jnp.minimum(lengths[source_of] - 1, most - lengths[taker]) // 2
    slack = jnp.where((source_of == sequence[0]) | (taker == sequence[0]) | (lengths[taker] == 0), 0, jnp.maximum(slack, 0))
    moved = jax.random.randint(jax.random.fold_in(own, 4), (number_of // 2,), 0, 1 << 20) % (slack + 1)
    lengths = lengths.at[source_of].add(-moved).at[taker].add(moved)
    items = jnp.searchsorted(jnp.cumsum(lengths), jnp.arange(rows * top), side="right").astype(jnp.int32)
    table = items.reshape(top, rows).T
    table = table[jax.random.permutation(jax.random.fold_in(own, 1), rows)]
    offset_by = jax.random.randint(jax.random.fold_in(own, 2), (rows, 1), 0, top)
    return jnp.take_along_axis(table, (jnp.arange(top)[None, :] + offset_by) % top, axis=1)


def portions_of(number_of, total, bound, lean, full):
    portions = [(1 << 20) // math.isqrt(grade ** lean) + 1 for grade in range(1, number_of + 1)]
    largest = bound if full else min(bound, max(-(-total // number_of), total * portions[0] // sum(portions)))
    least = 1 if total - largest >= number_of - 1 else 0
    counts, spare = [largest] + [least] * (number_of - 1), total - largest - least * (number_of - 1)
    while spare > 0:
        candidates = [i for i in range(1, number_of) if counts[i] < largest] or [i for i in range(1, number_of) if counts[i] < bound]
        pool, budget = sum([portions[i] for i in candidates]), spare
        for i in candidates:
            addition = min(bound - counts[i], max(1, budget * portions[i] // pool), spare)
            counts[i] = counts[i] + addition
            spare = spare - addition
    return np.array(counts)


def noise(key, extent, spread, reach, shards=(), kind=jnp.bfloat16):
    gain = shard_levels(key, extent, shards, -0.22, 0.18) if shards else 1.0
    drawn = jax.random.normal(key, extent, jnp.float32) * spread * gain
    return jnp.minimum(jnp.maximum(drawn, -reach), reach).astype(kind)


def setup_inputs(seed: int = 0) -> dict:
    seeds = jax.random.split(jax.random.key(seed), 8)
    tokens = noise(seeds[0], (TOKENS, D), 1.0, 6.0, ((0, 256),))
    cotangent = noise(seeds[1], (TOKENS, D), 1.0, 6.0, ((0, 256),))
    expert_ids_keys = jax.random.split(jax.random.fold_in(seeds[2], 1), TOKENS // TOK_DEV)
    expert_ids_turns = jax.random.permutation(jax.random.fold_in(seeds[2], 3), TOKENS // TOK_DEV)
    expert_ids = jax.vmap(lambda own, number: assign_block(jax.random.fold_in(seeds[2], 2), own, number, TOK_DEV, EXPERTS, TOPK, CAP, 2))(expert_ids_keys, expert_ids_turns).reshape((TOKENS, TOPK))
    gate_probs = jnp.clip(jnp.exp(math.log(1.0) - 2.9957323 * jax.random.uniform(seeds[3], (TOKENS, TOPK), jnp.float32) ** shard_levels(seeds[3], (TOKENS, TOPK), ((0, 256),), -0.2, 0.2)), 0.05, 1.0)
    w_gate = noise(seeds[4], (EXPERTS, D, FF), D ** -0.5, 0.125, ((0, 64), (1, 4)))
    w_up = noise(seeds[5], (EXPERTS, D, FF), D ** -0.5, 0.125, ((0, 64), (1, 4)))
    w_down = noise(seeds[6], (EXPERTS, FF, D), FF ** -0.5, 0.21875, ((0, 64), (1, 4)))
    return {"tokens": tokens, "cotangent": cotangent, "expert_ids": expert_ids, "gate_probs": gate_probs, "w_gate": w_gate, "w_up": w_up, "w_down": w_down}


def silu_parts(pre_gate):
    sigma = jax.nn.sigmoid(pre_gate)
    return pre_gate * sigma, sigma * (1.0 + pre_gate * (1.0 - sigma))


def rounded(values):
    return lax.optimization_barrier(values.astype(jnp.bfloat16)).astype(jnp.float32)


def reference(tokens, cotangent, expert_ids, gate_probs, w_gate, w_up, w_down):
    flat_ids = expert_ids.reshape(-1)
    flat_probs = gate_probs.reshape(-1)
    most_rows = CAP * DEVICES

    def per_expert(grad_acc, expert):
        hits = flat_ids == expert
        picked = jnp.nonzero(hits, size=most_rows, fill_value=0)[0].astype(jnp.int32)
        live = jnp.arange(most_rows, dtype=jnp.int32) < jnp.sum(hits.astype(jnp.int32))
        rows_at = picked // TOPK
        rows = tokens[rows_at].astype(jnp.float32)
        probs = jnp.where(live, flat_probs[picked], 0.0)
        scaled = rounded(probs[:, None] * cotangent[rows_at].astype(jnp.float32))
        gate_full = w_gate[expert].astype(jnp.float32)
        up_full = w_up[expert].astype(jnp.float32)
        down_full = w_down[expert].astype(jnp.float32)
        pre_gate = jnp.dot(rows, gate_full)
        pre_up = jnp.dot(rows, up_full)
        act_value, act_slope = silu_parts(pre_gate)
        activ = rounded(act_value * pre_up)
        grad_act = jnp.dot(scaled, down_full.T)
        grad_pre_gate = rounded(grad_act * pre_up * act_slope)
        grad_pre_up = rounded(grad_act * act_value)
        slot_grad = rounded(jnp.dot(grad_pre_gate, gate_full.T) + jnp.dot(grad_pre_up, up_full.T))
        grad_acc = grad_acc.at[rows_at].add(jnp.where(live[:, None], slot_grad, 0.0))
        sum_gate = jnp.dot(rows.T, grad_pre_gate).astype(jnp.bfloat16)
        sum_up = jnp.dot(rows.T, grad_pre_up).astype(jnp.bfloat16)
        sum_down = jnp.dot(activ.T, scaled).astype(jnp.bfloat16)
        return grad_acc, (sum_gate, sum_up, sum_down)

    start = jnp.zeros((TOKENS, D), jnp.float32)
    grad_acc, stacked = lax.scan(per_expert, start, jnp.arange(EXPERTS, dtype=jnp.int32))
    return grad_acc.astype(jnp.bfloat16), stacked[0], stacked[1], stacked[2]
```

```python
import jax
import jax.numpy as jnp
from jax import lax
from jax.sharding import PartitionSpec as P


def silu_parts(pre_gate):
    sigma = jax.nn.sigmoid(pre_gate)
    return (pre_gate * sigma, sigma * (1.0 + pre_gate * (1.0 - sigma)))


def shards(tokens, cotangent, expert_ids, gate_probs, w_gate, w_up, w_down):
    tok_rows, top_count = expert_ids.shape
    width = tokens.shape[1]
    owners = lax.axis_size("expert")
    slot_cap = (tok_rows * top_count * 9 + 8 * owners - 1) // (8 * owners)
    entries = tok_rows * top_count
    flat_ids = expert_ids.reshape(-1)
    one_hot = (flat_ids[:, None] == jnp.arange(owners, dtype=jnp.int32)[None, :]).astype(jnp.int32)
    ranks = jnp.sum((jnp.cumsum(one_hot, axis=0) - 1) * one_hot, axis=1)
    slots = flat_ids * slot_cap + ranks
    source = (
        jnp.zeros((owners * slot_cap,), jnp.int32)
        .at[slots]
        .set(jnp.arange(entries, dtype=jnp.int32) // top_count)
    )
    filled = jnp.zeros((owners * slot_cap,), jnp.bool_).at[slots].set(True)
    slot_probs = jnp.zeros((owners * slot_cap,), jnp.float32).at[slots].set(gate_probs.reshape(-1))
    send_rows = jnp.where(filled[:, None], tokens[source], jnp.zeros((), jnp.bfloat16))
    send_cot = (slot_probs[:, None] * cotangent[source].astype(jnp.float32)).astype(jnp.bfloat16)
    send_both = jnp.concatenate([send_rows, send_cot], axis=1).reshape(owners, slot_cap, 2 * width)
    full_gate, full_up, full_down = (
        lax.all_gather(w_gate, "dp", axis=1, tiled=True),
        lax.all_gather(w_up, "dp", axis=1, tiled=True),
        lax.all_gather(w_down, "dp", axis=1, tiled=True),
    )
    gate_full = full_gate[0]
    up_full = full_up[0]
    down_full = full_down[0]
    got_both = lax.all_to_all(send_both, "expert", split_axis=0, concat_axis=0, tiled=True)
    got_both = got_both.reshape(-1, 2 * width)
    rows = got_both[:, :width]
    scaled = got_both[:, width:]
    pre_gate = jnp.dot(rows, gate_full, preferred_element_type=jnp.float32)
    pre_up = jnp.dot(rows, up_full, preferred_element_type=jnp.float32)
    act_value, act_slope = silu_parts(pre_gate)
    activ = (act_value * pre_up).astype(jnp.bfloat16)
    grad_act = jnp.dot(scaled, down_full.T, preferred_element_type=jnp.float32)
    grad_pre_gate = (grad_act * pre_up * act_slope).astype(jnp.bfloat16)
    grad_pre_up = (grad_act * act_value).astype(jnp.bfloat16)
    part_gate = jnp.dot(rows.T, grad_pre_gate, preferred_element_type=jnp.float32)
    part_up = jnp.dot(rows.T, grad_pre_up, preferred_element_type=jnp.float32)
    part_down = jnp.dot(activ.T, scaled, preferred_element_type=jnp.float32)
    sum_gate, sum_up, sum_down = (
        lax.psum_scatter(part_gate.astype(jnp.bfloat16), "dp", scatter_dimension=0, tiled=True),
        lax.psum_scatter(part_up.astype(jnp.bfloat16), "dp", scatter_dimension=0, tiled=True),
        lax.psum_scatter(part_down.astype(jnp.bfloat16), "dp", scatter_dimension=0, tiled=True),
    )
    slot_grad = jnp.dot(grad_pre_gate, gate_full.T, preferred_element_type=jnp.float32)
    slot_grad = (
        slot_grad + jnp.dot(grad_pre_up, up_full.T, preferred_element_type=jnp.float32)
    ).astype(jnp.bfloat16)
    returned = lax.all_to_all(
        slot_grad.reshape(owners, slot_cap, width),
        "expert",
        split_axis=0,
        concat_axis=0,
        tiled=True,
    ).reshape(-1, width)
    per_entry = returned[slots].astype(jnp.float32).reshape(tok_rows, top_count, width)
    grad_tokens = jnp.sum(per_entry, axis=1).astype(jnp.bfloat16)
    return (
        grad_tokens,
        sum_gate[None],
        sum_up[None],
        sum_down[None],
    )


def solution(mesh):
    placed = (
        P(("expert", "dp"), None),
        P(("expert", "dp"), None),
        P(("expert", "dp"), None),
        P(("expert", "dp"), None),
        P("expert", "dp", None),
        P("expert", "dp", None),
        P("expert", "dp", None),
    )
    return jax.shard_map(
        shards,
        mesh=mesh,
        in_specs=placed,
        out_specs=(
            P(("expert", "dp"), None),
            P("expert", "dp", None),
            P("expert", "dp", None),
            P("expert", "dp", None),
        ),
        check_vma=False,
    )
```

```python
import jax
import jax.numpy as jnp
from jax import lax
from jax.sharding import PartitionSpec as P


def silu_parts(pre_gate):
    sigma = jax.nn.sigmoid(pre_gate)
    return (pre_gate * sigma, sigma * (1.0 + pre_gate * (1.0 - sigma)))


def shards(tokens, cotangent, expert_ids, gate_probs, w_gate, w_up, w_down):
    tok_rows, top_count = expert_ids.shape
    width = tokens.shape[1]
    owners = lax.axis_size("expert")
    slot_cap = (tok_rows * top_count * 9 + 8 * owners - 1) // (8 * owners)
    entries = tok_rows * top_count
    flat_ids = expert_ids.reshape(-1)
    one_hot = (flat_ids[:, None] == jnp.arange(owners, dtype=jnp.int32)[None, :]).astype(jnp.int32)
    ranks = jnp.sum((jnp.cumsum(one_hot, axis=0) - 1) * one_hot, axis=1)
    slots = flat_ids * slot_cap + ranks
    source = (
        jnp.zeros((owners * slot_cap,), jnp.int32)
        .at[slots]
        .set(jnp.arange(entries, dtype=jnp.int32) // top_count)
    )
    filled = jnp.zeros((owners * slot_cap,), jnp.bool_).at[slots].set(True)
    slot_probs = jnp.zeros((owners * slot_cap,), jnp.float32).at[slots].set(gate_probs.reshape(-1))
    send_rows = jnp.where(filled[:, None], tokens[source], jnp.zeros((), jnp.bfloat16))
    send_cot = (slot_probs[:, None] * cotangent[source].astype(jnp.float32)).astype(jnp.bfloat16)
    lanes = 128
    send_both = jnp.concatenate([send_rows, send_cot], axis=1).reshape(
        owners, slot_cap * 2 * width // lanes, lanes
    )
    full_gate, full_up, full_down = (
        lax.all_gather(w_gate, "dp", axis=1, tiled=True),
        lax.all_gather(w_up, "dp", axis=1, tiled=True),
        lax.all_gather(w_down, "dp", axis=1, tiled=True),
    )
    gate_full = full_gate[0]
    up_full = full_up[0]
    down_full = full_down[0]
    got_both = lax.all_to_all(send_both, "expert", split_axis=0, concat_axis=0, tiled=True)
    got_both = got_both.reshape(-1, 2 * width)
    rows = got_both[:, :width]
    scaled = got_both[:, width:]
    pre_gate = jnp.dot(rows, gate_full, preferred_element_type=jnp.float32)
    pre_up = jnp.dot(rows, up_full, preferred_element_type=jnp.float32)
    act_value, act_slope = silu_parts(pre_gate)
    activ = (act_value * pre_up).astype(jnp.bfloat16)
    grad_act = jnp.dot(scaled, down_full.T, preferred_element_type=jnp.float32)
    grad_pre_gate = (grad_act * pre_up * act_slope).astype(jnp.bfloat16)
    grad_pre_up = (grad_act * act_value).astype(jnp.bfloat16)
    part_gate = jnp.dot(rows.T, grad_pre_gate, preferred_element_type=jnp.float32)
    part_up = jnp.dot(rows.T, grad_pre_up, preferred_element_type=jnp.float32)
    part_down = jnp.dot(activ.T, scaled, preferred_element_type=jnp.float32)
    sum_gate, sum_up, sum_down = (
        lax.psum_scatter(part_gate.astype(jnp.bfloat16), "dp", scatter_dimension=0, tiled=True),
        lax.psum_scatter(part_up.astype(jnp.bfloat16), "dp", scatter_dimension=0, tiled=True),
        lax.psum_scatter(part_down.astype(jnp.bfloat16), "dp", scatter_dimension=0, tiled=True),
    )
    slot_grad = jnp.dot(grad_pre_gate, gate_full.T, preferred_element_type=jnp.float32)
    slot_grad = (
        slot_grad + jnp.dot(grad_pre_up, up_full.T, preferred_element_type=jnp.float32)
    ).astype(jnp.bfloat16)
    returned = lax.all_to_all(
        slot_grad.reshape(owners, slot_cap * width // lanes, lanes),
        "expert",
        split_axis=0,
        concat_axis=0,
        tiled=True,
    ).reshape(-1, width)
    per_entry = returned[slots].astype(jnp.float32).reshape(tok_rows, top_count, width)
    grad_tokens = jnp.sum(per_entry, axis=1).astype(jnp.bfloat16)
    return (
        grad_tokens,
        sum_gate[None],
        sum_up[None],
        sum_down[None],
    )


def solution(mesh):
    placed = (
        P(("expert", "dp"), None),
        P(("expert", "dp"), None),
        P(("expert", "dp"), None),
        P(("expert", "dp"), None),
        P("expert", "dp", None),
        P("expert", "dp", None),
        P("expert", "dp", None),
    )
    return jax.shard_map(
        shards,
        mesh=mesh,
        in_specs=placed,
        out_specs=(
            P(("expert", "dp"), None),
            P("expert", "dp", None),
            P("expert", "dp", None),
            P("expert", "dp", None),
        ),
        check_vma=False,
    )
```

```python
import jax
import jax.numpy as jnp
from jax import lax
from jax.experimental import pallas as pl
from jax.experimental.pallas import tpu as pltpu
from jax.sharding import PartitionSpec as P


def _exchange_kernel(send_ref, recv_ref, send_sems, recv_sems, local_sem):
    n = send_ref.shape[0]
    me = lax.axis_index("expert")
    group = lax.axis_index("dp")
    local = pltpu.make_async_copy(send_ref.at[me], recv_ref.at[me], local_sem.at[0])
    local.start()

    def remote(peer, slot):
        return pltpu.make_async_remote_copy(
            src_ref=send_ref.at[peer],
            dst_ref=recv_ref.at[slot],
            send_sem=send_sems.at[peer],
            recv_sem=recv_sems.at[slot],
            device_id=(peer, group),
            device_id_type=pl.DeviceIdType.MESH,
        )

    def start(i, carry):
        remote(lax.rem(me + i, n), me).start()
        return carry

    lax.fori_loop(1, n, start, 0)

    def wait(i, carry):
        remote(lax.rem(me + i, n), me).wait_send()
        src = lax.rem(me - i + n, n)
        remote(src, src).wait_recv()
        return carry

    lax.fori_loop(1, n, wait, 0)
    local.wait()


def exchange(x):
    n = x.shape[0]
    return pl.pallas_call(
        _exchange_kernel,
        out_shape=jax.ShapeDtypeStruct(x.shape, x.dtype),
        in_specs=[pl.BlockSpec(memory_space=pl.ANY)],
        out_specs=pl.BlockSpec(memory_space=pl.ANY),
        scratch_shapes=[
            pltpu.SemaphoreType.DMA((n,)),
            pltpu.SemaphoreType.DMA((n,)),
            pltpu.SemaphoreType.DMA((1,)),
        ],
        compiler_params=pltpu.CompilerParams(has_side_effects=True),
    )(x)


def silu_parts(pre_gate):
    sigma = jax.nn.sigmoid(pre_gate)
    return (pre_gate * sigma, sigma * (1.0 + pre_gate * (1.0 - sigma)))


def shards(tokens, cotangent, expert_ids, gate_probs, w_gate, w_up, w_down):
    tok_rows, top_count = expert_ids.shape
    width = tokens.shape[1]
    owners = lax.axis_size("expert")
    slot_cap = (tok_rows * top_count * 9 + 8 * owners - 1) // (8 * owners)
    entries = tok_rows * top_count
    flat_ids = expert_ids.reshape(-1)
    one_hot = (flat_ids[:, None] == jnp.arange(owners, dtype=jnp.int32)[None, :]).astype(jnp.int32)
    ranks = jnp.sum((jnp.cumsum(one_hot, axis=0) - 1) * one_hot, axis=1)
    slots = flat_ids * slot_cap + ranks
    source = (
        jnp.zeros((owners * slot_cap,), jnp.int32)
        .at[slots]
        .set(jnp.arange(entries, dtype=jnp.int32) // top_count)
    )
    filled = jnp.zeros((owners * slot_cap,), jnp.bool_).at[slots].set(True)
    slot_probs = jnp.zeros((owners * slot_cap,), jnp.float32).at[slots].set(gate_probs.reshape(-1))
    send_rows = jnp.where(filled[:, None], tokens[source], jnp.zeros((), jnp.bfloat16))
    send_cot = (slot_probs[:, None] * cotangent[source].astype(jnp.float32)).astype(jnp.bfloat16)
    lanes = 128
    send_both = jnp.concatenate([send_rows, send_cot], axis=1).reshape(
        owners, slot_cap * 2 * width // lanes, lanes
    )
    full_gate, full_up, full_down = (
        lax.all_gather(w_gate, "dp", axis=1, tiled=True),
        lax.all_gather(w_up, "dp", axis=1, tiled=True),
        lax.all_gather(w_down, "dp", axis=1, tiled=True),
    )
    gate_full = full_gate[0]
    up_full = full_up[0]
    down_full = full_down[0]
    got_both = exchange(send_both)
    got_both = got_both.reshape(-1, 2 * width)
    rows = got_both[:, :width]
    scaled = got_both[:, width:]
    pre_gate = jnp.dot(rows, gate_full, preferred_element_type=jnp.float32)
    pre_up = jnp.dot(rows, up_full, preferred_element_type=jnp.float32)
    act_value, act_slope = silu_parts(pre_gate)
    activ = (act_value * pre_up).astype(jnp.bfloat16)
    grad_act = jnp.dot(scaled, down_full.T, preferred_element_type=jnp.float32)
    grad_pre_gate = (grad_act * pre_up * act_slope).astype(jnp.bfloat16)
    grad_pre_up = (grad_act * act_value).astype(jnp.bfloat16)
    part_gate = jnp.dot(rows.T, grad_pre_gate, preferred_element_type=jnp.float32)
    part_up = jnp.dot(rows.T, grad_pre_up, preferred_element_type=jnp.float32)
    part_down = jnp.dot(activ.T, scaled, preferred_element_type=jnp.float32)
    sum_gate, sum_up, sum_down = (
        lax.psum_scatter(part_gate.astype(jnp.bfloat16), "dp", scatter_dimension=0, tiled=True),
        lax.psum_scatter(part_up.astype(jnp.bfloat16), "dp", scatter_dimension=0, tiled=True),
        lax.psum_scatter(part_down.astype(jnp.bfloat16), "dp", scatter_dimension=0, tiled=True),
    )
    slot_grad = jnp.dot(grad_pre_gate, gate_full.T, preferred_element_type=jnp.float32)
    slot_grad = (
        slot_grad + jnp.dot(grad_pre_up, up_full.T, preferred_element_type=jnp.float32)
    ).astype(jnp.bfloat16)
    returned = exchange(slot_grad.reshape(owners, slot_cap * width // lanes, lanes)).reshape(-1, width)
    per_entry = returned[slots].astype(jnp.float32).reshape(tok_rows, top_count, width)
    grad_tokens = jnp.sum(per_entry, axis=1).astype(jnp.bfloat16)
    return (
        grad_tokens,
        sum_gate[None],
        sum_up[None],
        sum_down[None],
    )


def solution(mesh):
    placed = (
        P(("expert", "dp"), None),
        P(("expert", "dp"), None),
        P(("expert", "dp"), None),
        P(("expert", "dp"), None),
        P("expert", "dp", None),
        P("expert", "dp", None),
        P("expert", "dp", None),
    )
    return jax.shard_map(
        shards,
        mesh=mesh,
        in_specs=placed,
        out_specs=(
            P(("expert", "dp"), None),
            P("expert", "dp", None),
            P("expert", "dp", None),
            P("expert", "dp", None),
        ),
        check_vma=False,
    )
```

```python
import jax
import jax.numpy as jnp
from jax import lax
from jax.sharding import PartitionSpec as P

LANES = 128


def silu_parts(pre_gate):
    sigma = jax.nn.sigmoid(pre_gate)
    return (pre_gate * sigma, sigma * (1.0 + pre_gate * (1.0 - sigma)))


def exchange(block):
    owners = block.shape[0]
    flat = block.reshape(owners, -1, LANES)
    got = lax.all_to_all(flat, "expert", split_axis=0, concat_axis=0, tiled=True)
    return got


def shards(tokens, cotangent, expert_ids, gate_probs, w_gate, w_up, w_down):
    tok_rows, top_count = expert_ids.shape
    width = tokens.shape[1]
    owners = lax.axis_size("expert")
    groups = lax.axis_size("dp")
    slot_cap = (tok_rows * top_count * 9 + 8 * owners - 1) // (8 * owners)
    flat_ids = expert_ids.reshape(-1)
    one_hot = (flat_ids[:, None] == jnp.arange(owners, dtype=jnp.int32)[None, :]).astype(jnp.int32)
    ranks = jnp.sum((jnp.cumsum(one_hot, axis=0) - 1) * one_hot, axis=1)
    slots = (flat_ids * slot_cap + ranks).reshape(tok_rows, top_count)
    picks = slots[None, :, :] == jnp.arange(owners * slot_cap, dtype=jnp.int32)[:, None, None]
    select = jnp.any(picks, axis=2).astype(jnp.bfloat16)
    slot_probs = jnp.sum(jnp.where(picks, gate_probs[None, :, :], 0.0), axis=(1, 2))
    send_rows = jnp.dot(select, tokens, preferred_element_type=jnp.float32).astype(jnp.bfloat16)
    send_cot = (
        slot_probs[:, None] * jnp.dot(select, cotangent, preferred_element_type=jnp.float32)
    ).astype(jnp.bfloat16)
    send_both = jnp.concatenate([send_rows, send_cot], axis=1).reshape(owners, slot_cap, 2 * width)
    full_gate, full_up, full_down = (
        lax.all_gather(w_gate, "dp", axis=1, tiled=True),
        lax.all_gather(w_up, "dp", axis=1, tiled=True),
        lax.all_gather(w_down, "dp", axis=1, tiled=True),
    )
    gate_full = full_gate[0]
    up_full = full_up[0]
    down_full = full_down[0]
    got_both = exchange(send_both).reshape(owners * slot_cap, 2 * width)
    rows = got_both[:, :width]
    scaled = got_both[:, width:]
    pre_gate = jnp.dot(rows, gate_full, preferred_element_type=jnp.float32)
    pre_up = jnp.dot(rows, up_full, preferred_element_type=jnp.float32)
    act_value, act_slope = silu_parts(pre_gate)
    activ = (act_value * pre_up).astype(jnp.bfloat16)
    grad_act = jnp.dot(scaled, down_full.T, preferred_element_type=jnp.float32)
    grad_pre_gate = (grad_act * pre_up * act_slope).astype(jnp.bfloat16)
    grad_pre_up = (grad_act * act_value).astype(jnp.bfloat16)
    part_gate = jnp.dot(rows.T, grad_pre_gate, preferred_element_type=jnp.float32)
    part_up = jnp.dot(rows.T, grad_pre_up, preferred_element_type=jnp.float32)
    part_down = jnp.dot(activ.T, scaled, preferred_element_type=jnp.float32)
    parts = (part_gate, part_up, part_down)
    packed = jnp.concatenate(
        [p.astype(jnp.bfloat16).reshape(groups, -1, LANES) for p in parts], axis=1
    )
    summed = lax.psum_scatter(packed, "dp", scatter_dimension=0, tiled=True)[0]
    sums = []
    start = 0
    for p in parts:
        length = p.size // groups // LANES
        sums.append(summed[start:start + length].reshape(1, -1, p.shape[1]))
        start += length
    sum_gate, sum_up, sum_down = sums
    slot_grad = jnp.dot(grad_pre_gate, gate_full.T, preferred_element_type=jnp.float32)
    slot_grad = (
        slot_grad + jnp.dot(grad_pre_up, up_full.T, preferred_element_type=jnp.float32)
    ).astype(jnp.bfloat16)
    returned = exchange(slot_grad.reshape(owners, slot_cap, width)).reshape(owners * slot_cap, width)
    grad_tokens = lax.dot_general(
        select, returned, (((0,), (0,)), ((), ())), preferred_element_type=jnp.float32
    ).astype(jnp.bfloat16)
    return (grad_tokens, sum_gate, sum_up, sum_down)


def solution(mesh):
    placed = (
        P(("expert", "dp"), None),
        P(("expert", "dp"), None),
        P(("expert", "dp"), None),
        P(("expert", "dp"), None),
        P("expert", "dp", None),
        P("expert", "dp", None),
        P("expert", "dp", None),
    )
    return jax.shard_map(
        shards,
        mesh=mesh,
        in_specs=placed,
        out_specs=(
            P(("expert", "dp"), None),
            P("expert", "dp", None),
            P("expert", "dp", None),
            P("expert", "dp", None),
        ),
        check_vma=False,
    )
```

```python
import jax
import jax.numpy as jnp
from jax import lax
from jax.sharding import PartitionSpec as P

LANES = 128


def silu_parts(pre_gate):
    sigma = jax.nn.sigmoid(pre_gate)
    return (pre_gate * sigma, sigma * (1.0 + pre_gate * (1.0 - sigma)))


def exchange(block):
    owners = block.shape[0]
    flat = block.reshape(owners, -1, LANES)
    got = lax.all_to_all(flat, "expert", split_axis=0, concat_axis=0, tiled=True)
    return got


def shards(tokens, cotangent, expert_ids, gate_probs, w_gate, w_up, w_down):
    tok_rows, top_count = expert_ids.shape
    width = tokens.shape[1]
    owners = lax.axis_size("expert")
    groups = lax.axis_size("dp")
    slot_cap = (tok_rows * top_count * 9 + 8 * owners - 1) // (8 * owners)
    flat_ids = expert_ids.reshape(-1)
    one_hot = (flat_ids[:, None] == jnp.arange(owners, dtype=jnp.int32)[None, :]).astype(jnp.int32)
    ranks = jnp.sum((jnp.cumsum(one_hot, axis=0) - 1) * one_hot, axis=1)
    slots = (flat_ids * slot_cap + ranks).reshape(tok_rows, top_count)
    picks = slots[None, :, :] == jnp.arange(owners * slot_cap, dtype=jnp.int32)[:, None, None]
    select = jnp.any(picks, axis=2).astype(jnp.bfloat16)
    slot_probs = jnp.sum(jnp.where(picks, gate_probs[None, :, :], 0.0), axis=(1, 2))
    send_rows = jnp.dot(select, tokens, preferred_element_type=jnp.float32).astype(jnp.bfloat16)
    send_cot = (
        slot_probs[:, None] * jnp.dot(select, cotangent, preferred_element_type=jnp.float32)
    ).astype(jnp.bfloat16)
    send_both = jnp.concatenate([send_rows, send_cot], axis=1).reshape(owners, slot_cap, 2 * width)
    full_gate, full_up, full_down = (
        lax.all_gather(w_gate, "dp", axis=1, tiled=True),
        lax.all_gather(w_up, "dp", axis=1, tiled=True),
        lax.all_gather(w_down, "dp", axis=1, tiled=True),
    )
    gate_full = full_gate[0]
    up_full = full_up[0]
    down_full = full_down[0]
    got_both = exchange(send_both).reshape(owners * slot_cap, 2 * width)
    rows = got_both[:, :width]
    scaled = got_both[:, width:]
    pre_gate = jnp.dot(rows, gate_full, preferred_element_type=jnp.float32)
    pre_up = jnp.dot(rows, up_full, preferred_element_type=jnp.float32)
    act_value, act_slope = silu_parts(pre_gate)
    activ = (act_value * pre_up).astype(jnp.bfloat16)
    grad_act = jnp.dot(scaled, down_full.T, preferred_element_type=jnp.float32)
    grad_pre_gate = (grad_act * pre_up * act_slope).astype(jnp.bfloat16)
    grad_pre_up = (grad_act * act_value).astype(jnp.bfloat16)
    grad_pre_both = jnp.concatenate([grad_pre_gate, grad_pre_up], axis=1)
    part_both = jnp.dot(rows.T, grad_pre_both, preferred_element_type=jnp.float32)
    part_down = jnp.dot(activ.T, scaled, preferred_element_type=jnp.float32)
    sum_down = lax.psum_scatter(part_down.astype(jnp.bfloat16), "dp", scatter_dimension=0, tiled=True)
    sum_both = lax.psum_scatter(part_both.astype(jnp.bfloat16), "dp", scatter_dimension=0, tiled=True)
    hidden = grad_pre_gate.shape[1]
    sum_gate = sum_both[:, :hidden][None]
    sum_up = sum_both[:, hidden:][None]
    sum_down = sum_down[None]
    slot_grad = jnp.dot(grad_pre_gate, gate_full.T, preferred_element_type=jnp.float32)
    slot_grad = (
        slot_grad + jnp.dot(grad_pre_up, up_full.T, preferred_element_type=jnp.float32)
    ).astype(jnp.bfloat16)
    returned = exchange(slot_grad.reshape(owners, slot_cap, width)).reshape(owners * slot_cap, width)
    grad_tokens = lax.dot_general(
        select, returned, (((0,), (0,)), ((), ())), preferred_element_type=jnp.float32
    ).astype(jnp.bfloat16)
    return (grad_tokens, sum_gate, sum_up, sum_down)


def solution(mesh):
    placed = (
        P(("expert", "dp"), None),
        P(("expert", "dp"), None),
        P(("expert", "dp"), None),
        P(("expert", "dp"), None),
        P("expert", "dp", None),
        P("expert", "dp", None),
        P("expert", "dp", None),
    )
    return jax.shard_map(
        shards,
        mesh=mesh,
        in_specs=placed,
        out_specs=(
            P(("expert", "dp"), None),
            P("expert", "dp", None),
            P("expert", "dp", None),
            P("expert", "dp", None),
        ),
        check_vma=False,
    )
```

```python
import jax
import jax.numpy as jnp
from jax import lax
from jax.sharding import PartitionSpec as P

LANES = 128


def silu_parts(pre_gate):
    sigma = jax.nn.sigmoid(pre_gate)
    return (pre_gate * sigma, sigma * (1.0 + pre_gate * (1.0 - sigma)))


def exchange(block):
    owners = block.shape[0]
    flat = block.reshape(owners, -1, LANES)
    got = lax.all_to_all(flat, "expert", split_axis=0, concat_axis=0, tiled=True)
    return got


def shards(tokens, cotangent, expert_ids, gate_probs, w_gate, w_up, w_down):
    tok_rows, top_count = expert_ids.shape
    width = tokens.shape[1]
    owners = lax.axis_size("expert")
    groups = lax.axis_size("dp")
    slot_cap = (tok_rows * top_count * 9 + 8 * owners - 1) // (8 * owners)
    flat_ids = expert_ids.reshape(-1)
    one_hot = (flat_ids[:, None] == jnp.arange(owners, dtype=jnp.int32)[None, :]).astype(jnp.int32)
    ranks = jnp.sum((jnp.cumsum(one_hot, axis=0) - 1) * one_hot, axis=1)
    slots = (flat_ids * slot_cap + ranks).reshape(tok_rows, top_count)
    picks = slots[None, :, :] == jnp.arange(owners * slot_cap, dtype=jnp.int32)[:, None, None]
    select = jnp.any(picks, axis=2).astype(jnp.bfloat16)
    slot_probs = jnp.sum(jnp.where(picks, gate_probs[None, :, :], 0.0), axis=(1, 2))
    send_rows = jnp.dot(select, tokens, preferred_element_type=jnp.float32).astype(jnp.bfloat16)
    send_cot = (
        slot_probs[:, None] * jnp.dot(select, cotangent, preferred_element_type=jnp.float32)
    ).astype(jnp.bfloat16)
    send_both = jnp.concatenate([send_rows, send_cot], axis=1).reshape(owners, slot_cap, 2 * width)
    full_gate, full_up, full_down = (
        lax.all_gather(w_gate, "dp", axis=1, tiled=True),
        lax.all_gather(w_up, "dp", axis=1, tiled=True),
        lax.all_gather(w_down, "dp", axis=1, tiled=True),
    )
    gate_full = full_gate[0]
    up_full = full_up[0]
    down_full = full_down[0]
    got_both = exchange(send_both).reshape(owners * slot_cap, 2 * width)
    rows = got_both[:, :width]
    scaled = got_both[:, width:]
    pre_gate = jnp.dot(rows, gate_full, preferred_element_type=jnp.float32)
    pre_up = jnp.dot(rows, up_full, preferred_element_type=jnp.float32)
    act_value, act_slope = silu_parts(pre_gate)
    activ = (act_value * pre_up).astype(jnp.bfloat16)
    part_down = jnp.dot(activ.T, scaled, preferred_element_type=jnp.float32).astype(jnp.bfloat16)
    sum_down = lax.psum_scatter(part_down, "dp", scatter_dimension=0, tiled=True)
    grad_act = jnp.dot(scaled, down_full.T, preferred_element_type=jnp.float32)
    grad_pre_gate = (grad_act * pre_up * act_slope).astype(jnp.bfloat16)
    grad_pre_up = (grad_act * act_value).astype(jnp.bfloat16)
    grad_pre_both = jnp.concatenate([grad_pre_gate, grad_pre_up], axis=1)
    part_both = jnp.dot(rows.T, grad_pre_both, preferred_element_type=jnp.float32)
    sum_both = lax.psum_scatter(part_both.astype(jnp.bfloat16), "dp", scatter_dimension=0, tiled=True)
    hidden = grad_pre_gate.shape[1]
    sum_gate = sum_both[:, :hidden][None]
    sum_up = sum_both[:, hidden:][None]
    sum_down = sum_down[None]
    slot_grad = jnp.dot(grad_pre_gate, gate_full.T, preferred_element_type=jnp.float32)
    slot_grad = (
        slot_grad + jnp.dot(grad_pre_up, up_full.T, preferred_element_type=jnp.float32)
    ).astype(jnp.bfloat16)
    sum_down, slot_grad = lax.optimization_barrier((sum_down, slot_grad))
    returned = exchange(slot_grad.reshape(owners, slot_cap, width)).reshape(owners * slot_cap, width)
    grad_tokens = lax.dot_general(
        select, returned, (((0,), (0,)), ((), ())), preferred_element_type=jnp.float32
    ).astype(jnp.bfloat16)
    return (grad_tokens, sum_gate, sum_up, sum_down)


def solution(mesh):
    placed = (
        P(("expert", "dp"), None),
        P(("expert", "dp"), None),
        P(("expert", "dp"), None),
        P(("expert", "dp"), None),
        P("expert", "dp", None),
        P("expert", "dp", None),
        P("expert", "dp", None),
    )
    return jax.shard_map(
        shards,
        mesh=mesh,
        in_specs=placed,
        out_specs=(
            P(("expert", "dp"), None),
            P("expert", "dp", None),
            P("expert", "dp", None),
            P("expert", "dp", None),
        ),
        check_vma=False,
    )
```

```python
import jax
import jax.numpy as jnp
from jax import lax
from jax.experimental import pallas as pl
from jax.experimental.pallas import tpu as pltpu
from jax.sharding import PartitionSpec as P

LANES = 128
XS = 4


def _exchange_kernel(send_ref, recv_ref, send_sems, recv_sems, local_sem):
    n = send_ref.shape[0]
    me = lax.axis_index("expert")
    group = lax.axis_index("dp")
    local = pltpu.make_async_copy(send_ref.at[me], recv_ref.at[me], local_sem.at[0])
    local.start()

    def remote(peer, slot):
        return pltpu.make_async_remote_copy(
            src_ref=send_ref.at[peer],
            dst_ref=recv_ref.at[slot],
            send_sem=send_sems.at[peer],
            recv_sem=recv_sems.at[slot],
            device_id=(peer, group),
            device_id_type=pl.DeviceIdType.MESH,
        )

    zs = n // (XS * 2)

    def offset(k):
        j = k % zs
        dz = jnp.where(j % 2 == 0, j // 2, zs - (j + 1) // 2)
        rest = k // zs
        return dz, rest // 2, rest % 2

    def peer_at(k, sign):
        dz, dx, dc = offset(k)
        z, x, c = me // (XS * 2), (me // 2) % XS, me % 2
        pz = (z + sign * dz + zs) % zs
        px = (x + sign * dx + XS) % XS
        pc = (c + sign * dc + 2) % 2
        return (pz * XS + px) * 2 + pc

    def start(k, carry):
        remote(peer_at(k, 1), me).start()
        return carry

    lax.fori_loop(1, n, start, 0)

    def wait(k, carry):
        remote(peer_at(k, 1), me).wait_send()
        src = peer_at(k, -1)
        remote(src, src).wait_recv()
        return carry

    lax.fori_loop(1, n, wait, 0)
    local.wait()


def exchange_kernel(x):
    n = x.shape[0]
    return pl.pallas_call(
        _exchange_kernel,
        out_shape=jax.ShapeDtypeStruct(x.shape, x.dtype),
        in_specs=[pl.BlockSpec(memory_space=pl.ANY)],
        out_specs=pl.BlockSpec(memory_space=pl.ANY),
        scratch_shapes=[
            pltpu.SemaphoreType.DMA((n,)),
            pltpu.SemaphoreType.DMA((n,)),
            pltpu.SemaphoreType.DMA((1,)),
        ],
        compiler_params=pltpu.CompilerParams(has_side_effects=True),
    )(x)


def silu_parts(pre_gate):
    sigma = jax.nn.sigmoid(pre_gate)
    return (pre_gate * sigma, sigma * (1.0 + pre_gate * (1.0 - sigma)))


def exchange(block):
    owners = block.shape[0]
    flat = block.reshape(owners, -1, LANES)
    got = lax.all_to_all(flat, "expert", split_axis=0, concat_axis=0, tiled=True)
    return got


def shards(tokens, cotangent, expert_ids, gate_probs, w_gate, w_up, w_down):
    tok_rows, top_count = expert_ids.shape
    width = tokens.shape[1]
    owners = lax.axis_size("expert")
    groups = lax.axis_size("dp")
    slot_cap = (tok_rows * top_count * 9 + 8 * owners - 1) // (8 * owners)
    flat_ids = expert_ids.reshape(-1)
    one_hot = (flat_ids[:, None] == jnp.arange(owners, dtype=jnp.int32)[None, :]).astype(jnp.int32)
    ranks = jnp.sum((jnp.cumsum(one_hot, axis=0) - 1) * one_hot, axis=1)
    slots = (flat_ids * slot_cap + ranks).reshape(tok_rows, top_count)
    picks = slots[None, :, :] == jnp.arange(owners * slot_cap, dtype=jnp.int32)[:, None, None]
    select = jnp.any(picks, axis=2).astype(jnp.bfloat16)
    slot_probs = jnp.sum(jnp.where(picks, gate_probs[None, :, :], 0.0), axis=(1, 2))
    send_rows = jnp.dot(select, tokens, preferred_element_type=jnp.float32).astype(jnp.bfloat16)
    send_cot = (
        slot_probs[:, None] * jnp.dot(select, cotangent, preferred_element_type=jnp.float32)
    ).astype(jnp.bfloat16)
    send_both = jnp.concatenate([send_rows, send_cot], axis=1).reshape(owners, slot_cap, 2 * width)
    full_gate, full_up, full_down = (
        lax.all_gather(w_gate, "dp", axis=1, tiled=True),
        lax.all_gather(w_up, "dp", axis=1, tiled=True),
        lax.all_gather(w_down, "dp", axis=1, tiled=True),
    )
    gate_full = full_gate[0]
    up_full = full_up[0]
    down_full = full_down[0]
    flat = send_both.reshape(owners, -1, LANES)
    got_both = exchange_kernel(flat).reshape(owners * slot_cap, 2 * width)
    rows = got_both[:, :width]
    scaled = got_both[:, width:]
    pre_gate = jnp.dot(rows, gate_full, preferred_element_type=jnp.float32)
    pre_up = jnp.dot(rows, up_full, preferred_element_type=jnp.float32)
    act_value, act_slope = silu_parts(pre_gate)
    activ = (act_value * pre_up).astype(jnp.bfloat16)
    grad_act = jnp.dot(scaled, down_full.T, preferred_element_type=jnp.float32)
    grad_pre_gate = (grad_act * pre_up * act_slope).astype(jnp.bfloat16)
    grad_pre_up = (grad_act * act_value).astype(jnp.bfloat16)
    grad_pre_both = jnp.concatenate([grad_pre_gate, grad_pre_up], axis=1)
    part_both = jnp.dot(rows.T, grad_pre_both, preferred_element_type=jnp.float32)
    part_down = jnp.dot(activ.T, scaled, preferred_element_type=jnp.float32)
    sum_down = lax.psum_scatter(part_down.astype(jnp.bfloat16), "dp", scatter_dimension=0, tiled=True)
    sum_both = lax.psum_scatter(part_both.astype(jnp.bfloat16), "dp", scatter_dimension=0, tiled=True)
    hidden = grad_pre_gate.shape[1]
    sum_gate = sum_both[:, :hidden][None]
    sum_up = sum_both[:, hidden:][None]
    sum_down = sum_down[None]
    slot_grad = jnp.dot(grad_pre_gate, gate_full.T, preferred_element_type=jnp.float32)
    slot_grad = (
        slot_grad + jnp.dot(grad_pre_up, up_full.T, preferred_element_type=jnp.float32)
    ).astype(jnp.bfloat16)
    returned = exchange(slot_grad.reshape(owners, slot_cap, width)).reshape(owners * slot_cap, width)
    grad_tokens = lax.dot_general(
        select, returned, (((0,), (0,)), ((), ())), preferred_element_type=jnp.float32
    ).astype(jnp.bfloat16)
    return (grad_tokens, sum_gate, sum_up, sum_down)


def solution(mesh):
    placed = (
        P(("expert", "dp"), None),
        P(("expert", "dp"), None),
        P(("expert", "dp"), None),
        P(("expert", "dp"), None),
        P("expert", "dp", None),
        P("expert", "dp", None),
        P("expert", "dp", None),
    )
    return jax.shard_map(
        shards,
        mesh=mesh,
        in_specs=placed,
        out_specs=(
            P(("expert", "dp"), None),
            P("expert", "dp", None),
            P("expert", "dp", None),
            P("expert", "dp", None),
        ),
        check_vma=False,
    )
```

```python
import jax
import jax.numpy as jnp
from jax import lax
from jax.experimental import pallas as pl
from jax.experimental.pallas import tpu as pltpu
from jax.sharding import PartitionSpec as P

LANES = 128


def _return_kernel(send_ref, down_ref, recv_ref, down_out, send_sems, recv_sems, y_send, y_recv, local_sems):
    n = send_ref.shape[0]
    groups = down_ref.shape[0]
    me = lax.axis_index("expert")
    group = lax.axis_index("dp")
    local = pltpu.make_async_copy(send_ref.at[me], recv_ref.at[me], local_sems.at[0])
    local.start()
    local_down = pltpu.make_async_copy(down_ref.at[group], down_out.at[group], local_sems.at[1])
    local_down.start()

    def remote(peer, slot):
        return pltpu.make_async_remote_copy(
            src_ref=send_ref.at[peer],
            dst_ref=recv_ref.at[slot],
            send_sem=send_sems.at[peer],
            recv_sem=recv_sems.at[slot],
            device_id=(peer, group),
            device_id_type=pl.DeviceIdType.MESH,
        )

    def across(target, slot):
        return pltpu.make_async_remote_copy(
            src_ref=down_ref.at[target],
            dst_ref=down_out.at[slot],
            send_sem=y_send.at[target],
            recv_sem=y_recv.at[slot],
            device_id=(me, target),
            device_id_type=pl.DeviceIdType.MESH,
        )

    def start_y(k, carry):
        across(lax.rem(group + k, groups), group).start()
        return carry

    lax.fori_loop(1, groups, start_y, 0)

    def start(i, carry):
        remote(lax.rem(me + i, n), me).start()
        return carry

    lax.fori_loop(1, n, start, 0)

    def wait_y(k, carry):
        across(lax.rem(group + k, groups), group).wait_send()
        src = lax.rem(group - k + groups, groups)
        across(src, src).wait_recv()
        return carry

    lax.fori_loop(1, groups, wait_y, 0)

    def wait(i, carry):
        remote(lax.rem(me + i, n), me).wait_send()
        src = lax.rem(me - i + n, n)
        remote(src, src).wait_recv()
        return carry

    lax.fori_loop(1, n, wait, 0)
    local.wait()
    local_down.wait()


def return_and_reduce(blocks, down_parts):
    n = blocks.shape[0]
    groups = down_parts.shape[0]
    return pl.pallas_call(
        _return_kernel,
        out_shape=(
            jax.ShapeDtypeStruct(blocks.shape, blocks.dtype),
            jax.ShapeDtypeStruct(down_parts.shape, down_parts.dtype),
        ),
        in_specs=[pl.BlockSpec(memory_space=pl.ANY)] * 2,
        out_specs=(pl.BlockSpec(memory_space=pl.ANY), pl.BlockSpec(memory_space=pl.ANY)),
        scratch_shapes=[
            pltpu.SemaphoreType.DMA((n,)),
            pltpu.SemaphoreType.DMA((n,)),
            pltpu.SemaphoreType.DMA((groups,)),
            pltpu.SemaphoreType.DMA((groups,)),
            pltpu.SemaphoreType.DMA((2,)),
        ],
        compiler_params=pltpu.CompilerParams(has_side_effects=True),
    )(blocks, down_parts)


def silu_parts(pre_gate):
    sigma = jax.nn.sigmoid(pre_gate)
    return (pre_gate * sigma, sigma * (1.0 + pre_gate * (1.0 - sigma)))


def exchange(block):
    owners = block.shape[0]
    flat = block.reshape(owners, -1, LANES)
    got = lax.all_to_all(flat, "expert", split_axis=0, concat_axis=0, tiled=True)
    return got


def shards(tokens, cotangent, expert_ids, gate_probs, w_gate, w_up, w_down):
    tok_rows, top_count = expert_ids.shape
    width = tokens.shape[1]
    owners = lax.axis_size("expert")
    groups = lax.axis_size("dp")
    slot_cap = (tok_rows * top_count * 9 + 8 * owners - 1) // (8 * owners)
    flat_ids = expert_ids.reshape(-1)
    one_hot = (flat_ids[:, None] == jnp.arange(owners, dtype=jnp.int32)[None, :]).astype(jnp.int32)
    ranks = jnp.sum((jnp.cumsum(one_hot, axis=0) - 1) * one_hot, axis=1)
    slots = (flat_ids * slot_cap + ranks).reshape(tok_rows, top_count)
    picks = slots[None, :, :] == jnp.arange(owners * slot_cap, dtype=jnp.int32)[:, None, None]
    select = jnp.any(picks, axis=2).astype(jnp.bfloat16)
    slot_probs = jnp.sum(jnp.where(picks, gate_probs[None, :, :], 0.0), axis=(1, 2))
    send_rows = jnp.dot(select, tokens, preferred_element_type=jnp.float32).astype(jnp.bfloat16)
    send_cot = (
        slot_probs[:, None] * jnp.dot(select, cotangent, preferred_element_type=jnp.float32)
    ).astype(jnp.bfloat16)
    send_both = jnp.concatenate([send_rows, send_cot], axis=1).reshape(owners, slot_cap, 2 * width)
    full_gate, full_up, full_down = (
        lax.all_gather(w_gate, "dp", axis=1, tiled=True),
        lax.all_gather(w_up, "dp", axis=1, tiled=True),
        lax.all_gather(w_down, "dp", axis=1, tiled=True),
    )
    gate_full = full_gate[0]
    up_full = full_up[0]
    down_full = full_down[0]
    got_both = exchange(send_both).reshape(owners * slot_cap, 2 * width)
    rows = got_both[:, :width]
    scaled = got_both[:, width:]
    pre_gate = jnp.dot(rows, gate_full, preferred_element_type=jnp.float32)
    pre_up = jnp.dot(rows, up_full, preferred_element_type=jnp.float32)
    act_value, act_slope = silu_parts(pre_gate)
    activ = (act_value * pre_up).astype(jnp.bfloat16)
    grad_act = jnp.dot(scaled, down_full.T, preferred_element_type=jnp.float32)
    grad_pre_gate = (grad_act * pre_up * act_slope).astype(jnp.bfloat16)
    grad_pre_up = (grad_act * act_value).astype(jnp.bfloat16)
    grad_pre_both = jnp.concatenate([grad_pre_gate, grad_pre_up], axis=1)
    part_both = jnp.dot(rows.T, grad_pre_both, preferred_element_type=jnp.float32)
    part_down = jnp.dot(activ.T, scaled, preferred_element_type=jnp.float32).astype(jnp.bfloat16)
    sum_both = lax.psum_scatter(part_both.astype(jnp.bfloat16), "dp", scatter_dimension=0, tiled=True)
    hidden = grad_pre_gate.shape[1]
    sum_gate = sum_both[:, :hidden][None]
    sum_up = sum_both[:, hidden:][None]
    slot_grad = jnp.dot(grad_pre_gate, gate_full.T, preferred_element_type=jnp.float32)
    slot_grad = (
        slot_grad + jnp.dot(grad_pre_up, up_full.T, preferred_element_type=jnp.float32)
    ).astype(jnp.bfloat16)
    returned, down_parts = return_and_reduce(
        slot_grad.reshape(owners, -1, LANES), part_down.reshape(groups, -1, part_down.shape[1])
    )
    returned = returned.reshape(owners * slot_cap, width)
    sum_down = jnp.sum(down_parts.astype(jnp.float32), axis=0).astype(jnp.bfloat16)[None]
    grad_tokens = lax.dot_general(
        select, returned, (((0,), (0,)), ((), ())), preferred_element_type=jnp.float32
    ).astype(jnp.bfloat16)
    return (grad_tokens, sum_gate, sum_up, sum_down)


def solution(mesh):
    placed = (
        P(("expert", "dp"), None),
        P(("expert", "dp"), None),
        P(("expert", "dp"), None),
        P(("expert", "dp"), None),
        P("expert", "dp", None),
        P("expert", "dp", None),
        P("expert", "dp", None),
    )
    return jax.shard_map(
        shards,
        mesh=mesh,
        in_specs=placed,
        out_specs=(
            P(("expert", "dp"), None),
            P("expert", "dp", None),
            P("expert", "dp", None),
            P("expert", "dp", None),
        ),
        check_vma=False,
    )
```

```python
import jax
import jax.numpy as jnp
from jax import lax
from jax.sharding import PartitionSpec as P

LANES = 128


def silu_parts(pre_gate):
    sigma = jax.nn.sigmoid(pre_gate)
    return (pre_gate * sigma, sigma * (1.0 + pre_gate * (1.0 - sigma)))


def exchange(block):
    owners = block.shape[0]
    flat = block.reshape(owners, -1, LANES)
    got = lax.all_to_all(flat, "expert", split_axis=0, concat_axis=0, tiled=True)
    return got


def shards(tokens, cotangent, expert_ids, gate_probs, w_gate, w_up, w_down):
    tok_rows, top_count = expert_ids.shape
    width = tokens.shape[1]
    owners = lax.axis_size("expert")
    groups = lax.axis_size("dp")
    slot_cap = (tok_rows * top_count * 9 + 8 * owners - 1) // (8 * owners)
    flat_ids = expert_ids.reshape(-1)
    one_hot = (flat_ids[:, None] == jnp.arange(owners, dtype=jnp.int32)[None, :]).astype(jnp.int32)
    ranks = jnp.sum((jnp.cumsum(one_hot, axis=0) - 1) * one_hot, axis=1)
    slots = (flat_ids * slot_cap + ranks).reshape(tok_rows, top_count)
    picks = slots[None, :, :] == jnp.arange(owners * slot_cap, dtype=jnp.int32)[:, None, None]
    select = jnp.any(picks, axis=2).astype(jnp.bfloat16)
    slot_probs = jnp.sum(jnp.where(picks, gate_probs[None, :, :], 0.0), axis=(1, 2))
    send_rows = jnp.dot(select, tokens, preferred_element_type=jnp.float32).astype(jnp.bfloat16)
    send_cot = (
        slot_probs[:, None] * jnp.dot(select, cotangent, preferred_element_type=jnp.float32)
    ).astype(jnp.bfloat16)
    send_both = jnp.concatenate([send_rows, send_cot], axis=1).reshape(owners, slot_cap, 2 * width)
    full_gate, full_up, full_down = (
        lax.all_gather(w_gate, "dp", axis=1, tiled=True),
        lax.all_gather(w_up, "dp", axis=1, tiled=True),
        lax.all_gather(w_down, "dp", axis=1, tiled=True),
    )
    gate_full = full_gate[0]
    up_full = full_up[0]
    down_full = full_down[0]
    got_both = exchange(send_both).reshape(owners * slot_cap, 2 * width)
    rows = got_both[:, :width]
    scaled = got_both[:, width:]
    pre_gate = jnp.dot(rows, gate_full, preferred_element_type=jnp.float32)
    pre_up = jnp.dot(rows, up_full, preferred_element_type=jnp.float32)
    act_value, act_slope = silu_parts(pre_gate)
    activ = (act_value * pre_up).astype(jnp.bfloat16)
    grad_act = jnp.dot(scaled, down_full.T, preferred_element_type=jnp.float32)
    grad_pre_gate = (grad_act * pre_up * act_slope).astype(jnp.bfloat16)
    grad_pre_up = (grad_act * act_value).astype(jnp.bfloat16)
    grad_pre_both = jnp.concatenate([grad_pre_gate, grad_pre_up], axis=1)
    part_both = jnp.dot(rows.T, grad_pre_both, preferred_element_type=jnp.float32)
    part_down = jnp.dot(activ.T, scaled, preferred_element_type=jnp.float32).astype(jnp.bfloat16)
    quarters = part_down.reshape(groups, -1, part_down.shape[1])
    mine = lax.axis_index("dp")
    sum_down = lax.dynamic_index_in_dim(quarters, mine, keepdims=False).astype(jnp.float32)
    for shift in range(1, groups):
        block = lax.dynamic_index_in_dim(quarters, (mine + shift) % groups, keepdims=False)
        ring = [(i, (i + shift) % groups) for i in range(groups)]
        sum_down = sum_down + lax.ppermute(block, "dp", ring).astype(jnp.float32)
    sum_both = lax.psum_scatter(part_both.astype(jnp.bfloat16), "dp", scatter_dimension=0, tiled=True)
    hidden = grad_pre_gate.shape[1]
    sum_gate = sum_both[:, :hidden][None]
    sum_up = sum_both[:, hidden:][None]
    sum_down = sum_down.astype(jnp.bfloat16)[None]
    slot_grad = jnp.dot(grad_pre_gate, gate_full.T, preferred_element_type=jnp.float32)
    slot_grad = (
        slot_grad + jnp.dot(grad_pre_up, up_full.T, preferred_element_type=jnp.float32)
    ).astype(jnp.bfloat16)
    returned = exchange(slot_grad.reshape(owners, slot_cap, width)).reshape(owners * slot_cap, width)
    grad_tokens = lax.dot_general(
        select, returned, (((0,), (0,)), ((), ())), preferred_element_type=jnp.float32
    ).astype(jnp.bfloat16)
    return (grad_tokens, sum_gate, sum_up, sum_down)


def solution(mesh):
    placed = (
        P(("expert", "dp"), None),
        P(("expert", "dp"), None),
        P(("expert", "dp"), None),
        P(("expert", "dp"), None),
        P("expert", "dp", None),
        P("expert", "dp", None),
        P("expert", "dp", None),
    )
    return jax.shard_map(
        shards,
        mesh=mesh,
        in_specs=placed,
        out_specs=(
            P(("expert", "dp"), None),
            P("expert", "dp", None),
            P("expert", "dp", None),
            P("expert", "dp", None),
        ),
        check_vma=False,
    )
```

```python
import jax
import jax.numpy as jnp
from jax import lax
from jax.sharding import PartitionSpec as P

LANES = 128


def silu_parts(pre_gate):
    sigma = jax.nn.sigmoid(pre_gate)
    return (pre_gate * sigma, sigma * (1.0 + pre_gate * (1.0 - sigma)))


def exchange(block):
    owners = block.shape[0]
    flat = block.reshape(owners, -1, LANES)
    got = lax.all_to_all(flat, "expert", split_axis=0, concat_axis=0, tiled=True)
    return got


def shards(tokens, cotangent, expert_ids, gate_probs, w_gate, w_up, w_down):
    tok_rows, top_count = expert_ids.shape
    width = tokens.shape[1]
    owners = lax.axis_size("expert")
    groups = lax.axis_size("dp")
    slot_cap = (tok_rows * top_count * 9 + 8 * owners - 1) // (8 * owners)
    flat_ids = expert_ids.reshape(-1)
    one_hot = (flat_ids[:, None] == jnp.arange(owners, dtype=jnp.int32)[None, :]).astype(jnp.int32)
    ranks = jnp.sum((jnp.cumsum(one_hot, axis=0) - 1) * one_hot, axis=1)
    slots = (flat_ids * slot_cap + ranks).reshape(tok_rows, top_count)
    picks = slots[None, :, :] == jnp.arange(owners * slot_cap, dtype=jnp.int32)[:, None, None]
    select = jnp.any(picks, axis=2).astype(jnp.bfloat16)
    slot_probs = jnp.sum(jnp.where(picks, gate_probs[None, :, :], 0.0), axis=(1, 2))
    send_rows = jnp.dot(select, tokens, preferred_element_type=jnp.float32).astype(jnp.bfloat16)
    send_cot = (
        slot_probs[:, None] * jnp.dot(select, cotangent, preferred_element_type=jnp.float32)
    ).astype(jnp.bfloat16)
    send_both = jnp.concatenate([send_rows, send_cot], axis=1).reshape(owners, slot_cap, 2 * width)
    hidden = w_gate.shape[2]
    gate_up = jnp.concatenate([w_gate[0], w_up[0]], axis=1)
    gu_full = lax.all_gather(gate_up, "dp", axis=0, tiled=True)
    down_full = lax.all_gather(w_down, "dp", axis=1, tiled=True)[0]
    got_both = exchange(send_both).reshape(owners * slot_cap, 2 * width)
    rows = got_both[:, :width]
    scaled = got_both[:, width:]
    pre_both = jnp.dot(rows, gu_full, preferred_element_type=jnp.float32)
    pre_gate = pre_both[:, :hidden]
    pre_up = pre_both[:, hidden:]
    act_value, act_slope = silu_parts(pre_gate)
    activ = (act_value * pre_up).astype(jnp.bfloat16)
    grad_act = jnp.dot(scaled, down_full.T, preferred_element_type=jnp.float32)
    grad_pre_gate = (grad_act * pre_up * act_slope).astype(jnp.bfloat16)
    grad_pre_up = (grad_act * act_value).astype(jnp.bfloat16)
    grad_pre_both = jnp.concatenate([grad_pre_gate, grad_pre_up], axis=1)
    part_both = jnp.dot(rows.T, grad_pre_both, preferred_element_type=jnp.float32)
    part_down = jnp.dot(activ.T, scaled, preferred_element_type=jnp.float32)
    sum_down = lax.psum_scatter(part_down.astype(jnp.bfloat16), "dp", scatter_dimension=0, tiled=True)
    sum_both = lax.psum_scatter(part_both.astype(jnp.bfloat16), "dp", scatter_dimension=0, tiled=True)
    sum_gate = sum_both[:, :hidden][None]
    sum_up = sum_both[:, hidden:][None]
    sum_down = sum_down[None]
    slot_grad = jnp.dot(grad_pre_both, gu_full.T, preferred_element_type=jnp.float32).astype(jnp.bfloat16)
    returned = exchange(slot_grad.reshape(owners, slot_cap, width)).reshape(owners * slot_cap, width)
    grad_tokens = lax.dot_general(
        select, returned, (((0,), (0,)), ((), ())), preferred_element_type=jnp.float32
    ).astype(jnp.bfloat16)
    return (grad_tokens, sum_gate, sum_up, sum_down)


def solution(mesh):
    placed = (
        P(("expert", "dp"), None),
        P(("expert", "dp"), None),
        P(("expert", "dp"), None),
        P(("expert", "dp"), None),
        P("expert", "dp", None),
        P("expert", "dp", None),
        P("expert", "dp", None),
    )
    return jax.shard_map(
        shards,
        mesh=mesh,
        in_specs=placed,
        out_specs=(
            P(("expert", "dp"), None),
            P("expert", "dp", None),
            P("expert", "dp", None),
            P("expert", "dp", None),
        ),
        check_vma=False,
    )
```

```python
import jax
import jax.numpy as jnp
from jax import lax
from jax.sharding import PartitionSpec as P

LANES = 128


def silu_parts(pre_gate):
    sigma = jax.nn.sigmoid(pre_gate)
    return (pre_gate * sigma, sigma * (1.0 + pre_gate * (1.0 - sigma)))


def exchange(block):
    owners = block.shape[0]
    flat = block.reshape(owners, -1, LANES)
    got = lax.all_to_all(flat, "expert", split_axis=0, concat_axis=0, tiled=True)
    return got


def shards(tokens, cotangent, expert_ids, gate_probs, w_gate, w_up, w_down):
    tok_rows, top_count = expert_ids.shape
    width = tokens.shape[1]
    owners = lax.axis_size("expert")
    groups = lax.axis_size("dp")
    slot_cap = (tok_rows * top_count * 9 + 8 * owners - 1) // (8 * owners)
    flat_ids = expert_ids.reshape(-1)
    one_hot = (flat_ids[:, None] == jnp.arange(owners, dtype=jnp.int32)[None, :]).astype(jnp.int32)
    ranks = jnp.sum((jnp.cumsum(one_hot, axis=0) - 1) * one_hot, axis=1)
    slots = (flat_ids * slot_cap + ranks).reshape(tok_rows, top_count)
    picks = slots[None, :, :] == jnp.arange(owners * slot_cap, dtype=jnp.int32)[:, None, None]
    select = jnp.any(picks, axis=2).astype(jnp.bfloat16)
    slot_probs = jnp.sum(jnp.where(picks, gate_probs[None, :, :], 0.0), axis=(1, 2))
    both = jnp.dot(
        select, jnp.concatenate([tokens, cotangent], axis=1), preferred_element_type=jnp.float32
    )
    scale = jnp.where(jnp.arange(2 * width) < width, 1.0, slot_probs[:, None])
    send_both = (both * scale).astype(jnp.bfloat16).reshape(owners, slot_cap, 2 * width)
    hidden = w_gate.shape[2]
    gate_up = jnp.concatenate([w_gate[0], w_up[0]], axis=1)
    gu_full = lax.all_gather(gate_up, "dp", axis=0, tiled=True)
    down_full = lax.all_gather(w_down, "dp", axis=1, tiled=True)[0]
    got_both = exchange(send_both).reshape(owners * slot_cap, 2 * width)
    rows = got_both[:, :width]
    scaled = got_both[:, width:]
    pre_both = jnp.dot(rows, gu_full, preferred_element_type=jnp.float32)
    pre_gate = pre_both[:, :hidden]
    pre_up = pre_both[:, hidden:]
    act_value, act_slope = silu_parts(pre_gate)
    activ = (act_value * pre_up).astype(jnp.bfloat16)
    grad_act = jnp.dot(scaled, down_full.T, preferred_element_type=jnp.float32)
    grad_pre_gate = (grad_act * pre_up * act_slope).astype(jnp.bfloat16)
    grad_pre_up = (grad_act * act_value).astype(jnp.bfloat16)
    grad_pre_both = jnp.concatenate([grad_pre_gate, grad_pre_up], axis=1)
    part_both = jnp.dot(rows.T, grad_pre_both, preferred_element_type=jnp.float32)
    part_down = jnp.dot(activ.T, scaled, preferred_element_type=jnp.float32)
    sum_down = lax.psum_scatter(part_down.astype(jnp.bfloat16), "dp", scatter_dimension=0, tiled=True)
    sum_both = lax.psum_scatter(part_both.astype(jnp.bfloat16), "dp", scatter_dimension=0, tiled=True)
    sum_gate = sum_both[:, :hidden][None]
    sum_up = sum_both[:, hidden:][None]
    sum_down = sum_down[None]
    slot_grad = jnp.dot(grad_pre_both, gu_full.T, preferred_element_type=jnp.float32).astype(jnp.bfloat16)
    returned = exchange(slot_grad.reshape(owners, slot_cap, width)).reshape(owners * slot_cap, width)
    grad_tokens = lax.dot_general(
        select, returned, (((0,), (0,)), ((), ())), preferred_element_type=jnp.float32
    ).astype(jnp.bfloat16)
    return (grad_tokens, sum_gate, sum_up, sum_down)


def solution(mesh):
    placed = (
        P(("expert", "dp"), None),
        P(("expert", "dp"), None),
        P(("expert", "dp"), None),
        P(("expert", "dp"), None),
        P("expert", "dp", None),
        P("expert", "dp", None),
        P("expert", "dp", None),
    )
    return jax.shard_map(
        shards,
        mesh=mesh,
        in_specs=placed,
        out_specs=(
            P(("expert", "dp"), None),
            P("expert", "dp", None),
            P("expert", "dp", None),
            P("expert", "dp", None),
        ),
        check_vma=False,
    )
```

```python
import jax
import jax.numpy as jnp
from jax import lax
from jax.sharding import PartitionSpec as P

LANES = 128


def silu_parts(pre_gate):
    sigma = jax.nn.sigmoid(pre_gate)
    return (pre_gate * sigma, sigma * (1.0 + pre_gate * (1.0 - sigma)))


def exchange(block):
    owners = block.shape[0]
    flat = block.reshape(owners, -1, LANES)
    got = lax.all_to_all(flat, "expert", split_axis=0, concat_axis=0, tiled=True)
    return got


def shards(tokens, cotangent, expert_ids, gate_probs, w_gate, w_up, w_down):
    tok_rows, top_count = expert_ids.shape
    width = tokens.shape[1]
    owners = lax.axis_size("expert")
    groups = lax.axis_size("dp")
    slot_cap = (tok_rows * top_count * 9 + 8 * owners - 1) // (8 * owners)
    flat_ids = expert_ids.reshape(-1)
    one_hot = (flat_ids[:, None] == jnp.arange(owners, dtype=jnp.int32)[None, :]).astype(jnp.int32)
    ranks = jnp.sum((jnp.cumsum(one_hot, axis=0) - 1) * one_hot, axis=1)
    slots = (flat_ids * slot_cap + ranks).reshape(tok_rows, top_count)
    picks = slots[None, :, :] == jnp.arange(owners * slot_cap, dtype=jnp.int32)[:, None, None]
    select = jnp.any(picks, axis=2).astype(jnp.bfloat16)
    slot_probs = jnp.sum(jnp.where(picks, gate_probs[None, :, :], 0.0), axis=(1, 2))
    send_rows = jnp.dot(select, tokens, preferred_element_type=jnp.float32).astype(jnp.bfloat16)
    send_cot = (
        slot_probs[:, None] * jnp.dot(select, cotangent, preferred_element_type=jnp.float32)
    ).astype(jnp.bfloat16)
    send_both = jnp.concatenate([send_rows, send_cot], axis=1).reshape(owners, slot_cap, 2 * width)
    hidden = w_gate.shape[2]
    gate_up = jnp.concatenate([w_gate[0], w_up[0]], axis=1)
    gu_full = lax.all_gather(gate_up, "dp", axis=0, tiled=True)
    down_full = lax.all_gather(w_down, "dp", axis=1, tiled=True)[0]
    got_both = exchange(send_both).reshape(owners * slot_cap, 2 * width)
    rows = got_both[:, :width]
    scaled = got_both[:, width:]
    pre_both = jnp.dot(rows, gu_full, preferred_element_type=jnp.float32)
    pre_gate = pre_both[:, :hidden]
    pre_up = pre_both[:, hidden:]
    act_value, act_slope = silu_parts(pre_gate)
    activ = (act_value * pre_up).astype(jnp.bfloat16)
    grad_act = jnp.dot(scaled, down_full.T, preferred_element_type=jnp.float32)
    grad_pre_gate = (grad_act * pre_up * act_slope).astype(jnp.bfloat16)
    grad_pre_up = (grad_act * act_value).astype(jnp.bfloat16)
    grad_pre_both = jnp.concatenate([grad_pre_gate, grad_pre_up], axis=1)
    part_both = jnp.dot(rows.T, grad_pre_both, preferred_element_type=jnp.float32)
    part_down = jnp.dot(activ.T, scaled, preferred_element_type=jnp.float32)
    sum_down = lax.psum_scatter(part_down.astype(jnp.bfloat16), "dp", scatter_dimension=0, tiled=True)
    sum_both = lax.psum_scatter(part_both.astype(jnp.bfloat16), "dp", scatter_dimension=0, tiled=True)
    sum_gate = sum_both[:, :hidden][None]
    sum_up = sum_both[:, hidden:][None]
    sum_down = sum_down[None]
    slot_grad = jnp.dot(grad_pre_both, gu_full.T, preferred_element_type=jnp.float32).astype(jnp.bfloat16)
    returned = exchange(slot_grad.reshape(owners, slot_cap, width)).reshape(owners * slot_cap, width)
    sum_down, returned = lax.optimization_barrier((sum_down, returned))
    grad_tokens = lax.dot_general(
        select, returned, (((0,), (0,)), ((), ())), preferred_element_type=jnp.float32
    ).astype(jnp.bfloat16)
    return (grad_tokens, sum_gate, sum_up, sum_down)


def solution(mesh):
    placed = (
        P(("expert", "dp"), None),
        P(("expert", "dp"), None),
        P(("expert", "dp"), None),
        P(("expert", "dp"), None),
        P("expert", "dp", None),
        P("expert", "dp", None),
        P("expert", "dp", None),
    )
    return jax.shard_map(
        shards,
        mesh=mesh,
        in_specs=placed,
        out_specs=(
            P(("expert", "dp"), None),
            P("expert", "dp", None),
            P("expert", "dp", None),
            P("expert", "dp", None),
        ),
        check_vma=False,
    )
```
